32 devices in a mesh: wide: 8 (over z, core), narrow: 4 (over y, x).
Axes of the slice: x: 2, y: 2, z: 4, core: 2. Of those that a mesh axis runs over, the one named last changes fastest.
Arguments:
- amplitudes: float32 [4, 64, 640, 640], P(None, 'wide', None, 'narrow'), may hold values from -6 to 6
- cycle_block: float32 [64, 640, 4, 640], P('wide', 'narrow'), may hold values from -0.078125 to 0.078125
- occupied_irreps: int32 [64], replicated, may hold values from 0 to 7, as said below
- virtual_irreps: int32 [640], replicated, may hold values from 0 to 7, as said below
- slab_orbitals: int32 [4], replicated, may hold values from 0 to 63, as said below
Outputs:
- cycle_residual: float32 [4, 4, 640, 640], P(None, None, 'narrow', 'wide')
The draws below stay inside these ranges and needn't reach their ends.
Inputs may be any that keep to these rules, and one draw needn't show every extreme that they name: `occupied_irreps`: nondecreasing; every irrep 0 to 7 labels at least 4 orbitals. `virtual_irreps`: nondecreasing; every irrep 0 to 7 labels at least 64 orbitals. `slab_orbitals`: distinct occupied orbital indices in increasing order; the last is 63.
All inputs are finite; a program needn't handle non-finite values.
Results may differ from the reference program's by a relative error of at most 0.0003.
Values sent between devices are 32-bit elements; how exact they have to be, the bound alone decides.
A program may use at most 192 MiB of HBM per device.

```python
import jax
import jax.numpy as jnp
from jax import lax

O = 64
V = 640
NI = 4
OBLK = 4
VBLK = 64


def draw_labels(key, count, least):
    base = jnp.repeat(jnp.arange(8, dtype=jnp.int32), least)
    extra = jax.random.randint(key, (count - 8 * least,), 0, 8, dtype=jnp.int32)
    return jnp.sort(jnp.concatenate([base, extra])).astype(jnp.int32)


def draw_occupied_irreps(key, part):
    return draw_labels(jax.random.fold_in(key, 11), O, OBLK)


def draw_virtual_irreps(key, part):
    return draw_labels(jax.random.fold_in(key, 12), V, VBLK)


def draw_slab_orbitals(key, part):
    order = jax.random.permutation(jax.random.fold_in(key, 13), O - 1).astype(jnp.int32)
    chosen = jnp.sort(order[:NI - 1]).astype(jnp.int32)
    last = jnp.full((1,), O - 1, dtype=jnp.int32)
    return jnp.concatenate([chosen, last]).astype(jnp.int32)


def levels(own_key, shape, cuts, low, high):
    def one(position, blocks):
        steps = jax.random.uniform(jax.random.fold_in(jax.random.fold_in(own_key, 6), position), (blocks,), jnp.float32, low / len(cuts), high / len(cuts))
        return jnp.repeat(jnp.exp(steps), shape[position] // blocks).reshape((-1,) + (1,) * (len(shape) - position - 1))

    loudness = one(*cuts[0])
    for cut in cuts[1:]:
        loudness = loudness * one(*cut)
    return loudness


def noise(own_key, shape, scale, bound, shards=(), kind=jnp.bfloat16):
    result = scale * jax.random.normal(own_key, shape, jnp.float32)
    if shards:
        result = result * levels(own_key, shape, shards, -0.22, 0.18)
    return jnp.clip(result, -bound, bound).astype(kind)


def setup_inputs(seed: int = 0) -> dict:
    splits = jax.random.split(jax.random.key(seed), 6)
    return {
        "amplitudes": noise(splits[0], (NI, O, V, V), 1.0, 6.0, ((1, 8), (3, 4)), jnp.float32),
        "cycle_block": noise(splits[1], (O, V, NI, V), (O * V // 8) ** -0.5, 0.078125, ((0, 8), (1, 4)), jnp.float32),
        "occupied_irreps": draw_occupied_irreps(jax.random.fold_in(splits[5], 71), 0),
        "virtual_irreps": draw_virtual_irreps(jax.random.fold_in(splits[5], 71), 0),
        "slab_orbitals": draw_slab_orbitals(jax.random.fold_in(splits[5], 71), 0),
    }


def select_sym(values, first, second, third, fourth):
    labels = jnp.bitwise_xor(jnp.bitwise_xor(first[:, None, None, None], second[None, :, None, None]), jnp.bitwise_xor(third[None, None, :, None], fourth[None, None, None, :]))
    return jnp.where(labels == 0, values, jnp.zeros_like(values))


def reference(amplitudes, cycle_block, occupied_irreps, virtual_irreps, slab_orbitals):
    orbits = jnp.arange(occupied_irreps.shape[0], dtype=jnp.int32)
    slab_irreps = jnp.sum(jnp.where(orbits[None, :] == slab_orbitals[:, None], occupied_irreps[None, :], 0), axis=1).astype(jnp.int32)
    kept_cycle = select_sym(cycle_block, occupied_irreps, virtual_irreps, slab_irreps, virtual_irreps)

    def single(pair):
        row, label = pair
        kept = select_sym(row[None], label[None], occupied_irreps, virtual_irreps, virtual_irreps)[0]
        return jnp.einsum("kac,kcjb->jab", kept, kept_cycle, precision=lax.Precision.HIGHEST)

    return lax.map(single, (amplitudes, slab_irreps))
```

```python
import functools

import jax
import jax.numpy as jnp
from jax import lax
from jax.experimental import pallas as pl
from jax.experimental.pallas import tpu as pltpu
from jax.sharding import PartitionSpec as P

IRREPS = 8
ROWS = 8
FEWEST = 64


def split(x):
    high = x.astype(jnp.bfloat16)
    low = (x - high.astype(jnp.float32)).astype(jnp.bfloat16)
    return high, low


def mm(x, y):
    return jnp.dot(x, y, preferred_element_type=jnp.float32)


def contract(cap, wide, tab, a_ref, w_ref, hc_row, hc_col, hb_row, out_ref, acc, rows):
    k = pl.program_id(0)
    n_k = pl.num_programs(0)
    ni = a_ref.shape[0]
    nb = w_ref.shape[3]
    bw = nb // wide
    hk = tab[ni + k]
    base = ni + n_k
    first, last = tab[base + IRREPS], tab[base + IRREPS + 1]
    c_labels = hc_row[...]
    for i in range(ni):
        g = tab[i] ^ hk

        def pick(h, kept):
            block = a_ref[i, 0, pl.ds(pl.multiple_of(tab[base + (h ^ g)], ROWS), cap), :]
            return jnp.where(c_labels == h, block, kept)

        rows[i * cap : (i + 1) * cap, :] = lax.fori_loop(
            first, last + 1, pick, jnp.zeros((cap, a_ref.shape[3]), jnp.float32)
        )
    l_hi, l_lo = split(rows[...])
    labels = hc_col[...] ^ hb_row[...]
    w_all = jnp.swapaxes(w_ref[0], 0, 1)
    for j in range(ni):
        w = jnp.where(labels == (tab[j] ^ hk), w_all[j], 0.0)
        w_hi, w_lo = split(w)
        term = mm(l_hi, w_hi) + mm(l_hi, w_lo) + mm(l_lo, w_hi)

        @pl.when(k == 0)
        def _():
            acc[j] = term

        @pl.when(k > 0)
        def _():
            acc[j] += term

    @pl.when(k == n_k - 1)
    def _():
        for j in range(ni):
            turned = acc[j].T
            for w in range(wide):
                out_ref[(w * ni + j) * bw : (w * ni + j + 1) * bw, :] = turned[w * bw : (w + 1) * bw]


def unpack(cap, tab, g_ref, hb_row, out_ref, buf):
    ni, _, na, bw = out_ref.shape
    buf[...] = jnp.zeros_like(buf)
    first, last, a0 = (tab[ni + 3 * IRREPS + n] for n in range(3))
    labels = hb_row[...]
    at = a0 + lax.broadcasted_iota(jnp.int32, (na, bw), 0)
    for j in range(ni):
        turned = g_ref[j * bw : (j + 1) * bw, :].T
        for i in range(ni):
            buf[na : na + cap, :] = turned[i * cap : (i + 1) * cap]
            g = tab[i] ^ tab[j]

            def place(h, kept):
                block = h ^ g
                start = jnp.clip(na + a0 - tab[ni + block], 0, na + cap)
                low, high = tab[ni + IRREPS + block], tab[ni + 2 * IRREPS + block]
                use = (labels == h) & (at >= low) & (at < high)
                return jnp.where(use, buf[pl.ds(pl.multiple_of(start, ROWS), na), :], kept)

            out_ref[i, j] = lax.fori_loop(first, last + 1, place, jnp.zeros((na, bw), jnp.float32))


def local(amplitudes, cycle_block, occupied_irreps, virtual_irreps, slab_orbitals):
    ni, n_k, va, nc = amplitudes.shape
    vb = cycle_block.shape[3]
    wide, narrow = lax.axis_size("wide"), lax.axis_size("narrow")
    wide_pos, narrow_pos = lax.axis_index("wide"), lax.axis_index("narrow")
    bw, na = vb // wide, va // narrow
    most = va - (IRREPS - 1) * FEWEST
    cap = most // 2

    slab = jnp.sum(
        jnp.where(
            jnp.arange(occupied_irreps.shape[0], dtype=jnp.int32)[None, :] == slab_orbitals[:, None],
            occupied_irreps[None, :],
            0,
        ),
        axis=1,
    )
    occ_part = lax.dynamic_slice_in_dim(occupied_irreps, wide_pos * n_k, n_k)
    c_part = lax.dynamic_slice_in_dim(virtual_irreps, narrow_pos * nc, nc)
    b_part = lax.dynamic_slice_in_dim(virtual_irreps, wide_pos * bw, bw)
    names = jnp.arange(IRREPS, dtype=jnp.int32)
    starts = jnp.sum((virtual_irreps[None, :] < names[:, None]).astype(jnp.int32), axis=1)
    aligned = starts // ROWS * ROWS
    ends = jnp.concatenate([starts[1:], jnp.full((1,), va, jnp.int32)])

    def part(offset):
        packed = jnp.minimum(aligned + offset, va - cap)
        tab = jnp.concatenate([slab, occ_part, packed, c_part[:1], c_part[-1:]])
        partial_sums = pl.pallas_call(
            functools.partial(contract, cap, wide),
            out_shape=jax.ShapeDtypeStruct((ni * vb, ni * cap), jnp.float32),
            grid_spec=pltpu.PrefetchScalarGridSpec(
                num_scalar_prefetch=1,
                grid=(n_k,),
                in_specs=[
                    pl.BlockSpec((ni, 1, va, nc), lambda k, t: (0, k, 0, 0)),
                    pl.BlockSpec((1, nc, ni, vb), lambda k, t: (k, 0, 0, 0)),
                    pl.BlockSpec((1, nc), lambda k, t: (0, 0)),
                    pl.BlockSpec((nc, 1), lambda k, t: (0, 0)),
                    pl.BlockSpec((1, vb), lambda k, t: (0, 0)),
                ],
                out_specs=pl.BlockSpec((ni * vb, ni * cap), lambda k, t: (0, 0)),
                scratch_shapes=[
                    pltpu.VMEM((ni, ni * cap, vb), jnp.float32),
                    pltpu.VMEM((ni * cap, nc), jnp.float32),
                ],
            ),
            compiler_params=pltpu.CompilerParams(vmem_limit_bytes=60 * 2**20),
        )(tab, amplitudes, cycle_block, c_part[None, :], c_part[:, None], virtual_irreps[None, :])
        mine = lax.psum_scatter(partial_sums, ("wide", "narrow"), scatter_dimension=0, tiled=True)
        summed = lax.all_gather(mine, "narrow", axis=0, tiled=True)
        low = jnp.maximum(aligned + offset, starts)
        high = jnp.minimum(aligned + offset + cap, ends)
        tab = jnp.concatenate([slab, packed, low, high, b_part[:1], b_part[-1:], (narrow_pos * na)[None]])
        return pl.pallas_call(
            functools.partial(unpack, cap),
            out_shape=jax.ShapeDtypeStruct((ni, ni, na, bw), jnp.float32),
            grid_spec=pltpu.PrefetchScalarGridSpec(
                num_scalar_prefetch=1,
                grid=(1,),
                in_specs=[
                    pl.BlockSpec((ni * bw, ni * cap), lambda k, t: (0, 0)),
                    pl.BlockSpec((1, bw), lambda k, t: (0, 0)),
                ],
                out_specs=pl.BlockSpec((ni, ni, na, bw), lambda k, t: (0, 0, 0, 0)),
                scratch_shapes=[pltpu.VMEM((2 * na + cap, bw), jnp.float32)],
            ),
        )(tab, summed, b_part[None, :])

    first = part(0)
    return lax.cond(jnp.max(ends - aligned) > cap, lambda x: x + part(cap), lambda x: x, first)


def solution(mesh):
    placed = (P(None, "wide", None, "narrow"), P("wide", "narrow", None, None), P(), P(), P())
    return jax.shard_map(
        local,
        mesh=mesh,
        in_specs=placed,
        out_specs=P(None, None, "narrow", "wide"),
        check_vma=False,
    )
```

```python
import functools

import jax
import jax.numpy as jnp
from jax import lax
from jax.experimental import pallas as pl
from jax.experimental.pallas import tpu as pltpu
from jax.sharding import PartitionSpec as P

IRREPS = 8
CORES = 2
LANES = 128
ROWS = 8
FEWEST = 64


def split(x):
    high = x.astype(jnp.bfloat16)
    low = (x - high.astype(jnp.float32)).astype(jnp.bfloat16)
    return high, low


def mm(x, y):
    return jnp.dot(x, y, preferred_element_type=jnp.float32)


def contract(cap, tab, a_ref, w_ref, hc_row, hc_col, hb_row, out_ref, acc, turn, rows, deep_l, deep_w):
    k = pl.program_id(0)
    n_k = pl.num_programs(0)
    ni, nc = a_ref.shape[0], a_ref.shape[2]
    cores, zs, narrow, nr, _ = out_ref.shape
    hk = tab[ni + k]
    base = ni + n_k
    first, last = tab[base + IRREPS], tab[base + IRREPS + 1]
    c_labels = hc_row[...]
    for i in range(ni):
        g = tab[i] ^ hk
        turn[i] = a_ref[i, 0].T

        def pick(h, kept):
            start = pl.multiple_of(tab[base + (h ^ g)], ROWS)
            return jnp.where(c_labels == h, turn[i, pl.ds(start, cap), :], kept)

        rows[i * cap : (i + 1) * cap, :] = lax.fori_loop(first, last + 1, pick, jnp.zeros((cap, nc), jnp.float32))
    l_hi, l_lo = split(rows[...])
    joined = nc % 16 == 0
    if joined:
        deep_l[:, :nc] = l_hi
        deep_l[:, nc : 2 * nc] = l_hi
        deep_l[:, 2 * nc :] = l_lo
    labels = hc_col[...] ^ hb_row[...]
    w_all = jnp.swapaxes(w_ref[0], 0, 1)
    for j in range(ni):
        w_hi, w_lo = split(jnp.where(labels == (tab[j] ^ hk), w_all[j], 0.0))
        if joined:
            deep_w[j, :nc] = w_hi
            deep_w[j, nc : 2 * nc] = w_lo
            deep_w[j, 2 * nc :] = w_hi
            term = mm(deep_l[...], deep_w[j])
        else:
            term = mm(l_hi, w_hi) + mm(l_hi, w_lo) + mm(l_lo, w_hi)

        @pl.when(k == 0)
        def _():
            acc[j] = term

        @pl.when(k > 0)
        def _():
            acc[j] += term

    @pl.when(k == n_k - 1)
    def _():
        pieces = narrow // ni
        for j in range(ni):
            turned = acc[j].T
            for n in range(cores * zs * pieces):
                w, piece = divmod(n, pieces)
                out_ref[w % cores, w // cores, j * pieces + piece] = turned[n * nr : (n + 1) * nr]


def exchange(q_ref, out_ref, cbuf, s1, nbuf, s2, zbuf, gbuf, csem, nsend, nrecv, zsend, zrecv, gsend, grecv):
    cores, zs, narrow, _, lanes = q_ref.shape
    wide_pos, n = lax.axis_index("wide"), lax.axis_index("narrow")
    z, core = wide_pos // cores, lax.rem(wide_pos, cores)
    other = 1 - core
    partner = (z * cores + other, n)
    n_peers = [lax.rem(n + d, narrow) for d in range(1, narrow)]
    z_peers = [lax.rem(z + d, zs) for d in range(1, zs)]

    def at_n(p):
        return (wide_pos, p)

    def at_z(p):
        return (p * cores + core, n)

    barrier = pltpu.get_barrier_semaphore()
    peers = [partner] + [at_n(p) for p in n_peers] + [at_z(p) for p in z_peers]
    for peer in peers:
        pl.semaphore_signal(barrier, inc=1, device_id=peer, device_id_type=pl.DeviceIdType.MESH)
    pl.semaphore_wait(barrier, len(peers))

    def copy(src, dst, send, recv, device):
        return pltpu.make_async_remote_copy(
            src_ref=src, dst_ref=dst, send_sem=send, recv_sem=recv, device_id=device, device_id_type=pl.DeviceIdType.MESH
        )

    groups = [(g, pl.ds(g * LANES, LANES)) for g in range(lanes // LANES)]
    sent = []

    def push(c):
        c.start()
        sent.append(c)

    for g, part in groups:
        push(copy(q_ref.at[other, :, :, :, part], cbuf.at[:, :, :, part], csem.at[0, g], csem.at[1, g], partner))
    for g, part in groups:
        sent[g].wait_recv()
        s1[:, :, :, part] = q_ref[core, :, :, :, part] + cbuf[:, :, :, part]
        for p in n_peers:
            push(copy(s1.at[:, p, :, part], nbuf.at[n, :, :, part], nsend.at[p, g], nrecv.at[n, g], at_n(p)))
    for g, part in groups:
        total = s1[:, n, :, part]
        for p in n_peers:
            copy(s1.at[:, p, :, part], nbuf.at[p, :, :, part], nsend.at[p, g], nrecv.at[p, g], at_n(p)).wait_recv()
            total = total + nbuf[p, :, :, part]
        s2[:, :, part] = total
        for p in z_peers:
            push(copy(s2.at[p, :, part], zbuf.at[z, :, part], zsend.at[p, g], zrecv.at[z, g], at_z(p)))
    for g, part in groups:
        total = s2[z, :, part]
        for p in z_peers:
            copy(s2.at[p, :, part], zbuf.at[p, :, part], zsend.at[p, g], zrecv.at[p, g], at_z(p)).wait_recv()
            total = total + zbuf[p, :, part]
        gbuf[n, :, part] = total
        for p in n_peers:
            push(copy(gbuf.at[n, :, part], gbuf.at[n, :, part], gsend.at[p, g], grecv.at[n, g], at_n(p)))
    for g, part in groups:
        for p in n_peers:
            copy(gbuf.at[n, :, part], gbuf.at[p, :, part], gsend.at[p, g], grecv.at[p, g], at_n(p)).wait_recv()
    for c in sent:
        c.wait_send()
    out_ref[...] = gbuf[...]


def unpack(cap, tab, g_ref, hb_row, out_ref, buf):
    ni, _, na, bw = out_ref.shape
    buf[...] = jnp.zeros_like(buf)
    first, last, a0 = (tab[ni + 3 * IRREPS + n] for n in range(3))
    labels = hb_row[...]
    at = a0 + lax.broadcasted_iota(jnp.int32, (na, bw), 0)
    for j in range(ni):
        turned = g_ref[j * bw : (j + 1) * bw, :].T
        for i in range(ni):
            buf[na : na + cap, :] = turned[i * cap : (i + 1) * cap]
            g = tab[i] ^ tab[j]

            def place(h, kept):
                block = h ^ g
                start = jnp.clip(na + a0 - tab[ni + block], 0, na + cap)
                low, high = tab[ni + IRREPS + block], tab[ni + 2 * IRREPS + block]
                use = (labels == h) & (at >= low) & (at < high)
                return jnp.where(use, buf[pl.ds(pl.multiple_of(start, ROWS), na), :], kept)

            out_ref[i, j] = lax.fori_loop(first, last + 1, place, jnp.zeros((na, bw), jnp.float32))


def local(amplitudes, cycle_block, occupied_irreps, virtual_irreps, slab_orbitals):
    ni, n_k, va, nc = amplitudes.shape
    vb = cycle_block.shape[3]
    wide, narrow = lax.axis_size("wide"), lax.axis_size("narrow")
    wide_pos, narrow_pos = lax.axis_index("wide"), lax.axis_index("narrow")
    bw, na = vb // wide, va // narrow
    most = va - (IRREPS - 1) * FEWEST
    cap = most // 2
    blocks = (CORES, wide // CORES, narrow, ni * bw // narrow, ni * cap)

    slab = jnp.sum(
        jnp.where(
            jnp.arange(occupied_irreps.shape[0], dtype=jnp.int32)[None, :] == slab_orbitals[:, None],
            occupied_irreps[None, :],
            0,
        ),
        axis=1,
    )
    occ_part = lax.dynamic_slice_in_dim(occupied_irreps, wide_pos * n_k, n_k)
    c_part = lax.dynamic_slice_in_dim(virtual_irreps, narrow_pos * nc, nc)
    b_part = lax.dynamic_slice_in_dim(virtual_irreps, wide_pos * bw, bw)
    names = jnp.arange(IRREPS, dtype=jnp.int32)
    starts = jnp.sum((virtual_irreps[None, :] < names[:, None]).astype(jnp.int32), axis=1)
    aligned = starts // ROWS * ROWS
    ends = jnp.concatenate([starts[1:], jnp.full((1,), va, jnp.int32)])

    def part(offset):
        packed = jnp.minimum(aligned + offset, va - cap)
        tab = jnp.concatenate([slab, occ_part, packed, c_part[:1], c_part[-1:]])
        partial_sums = pl.pallas_call(
            functools.partial(contract, cap),
            out_shape=jax.ShapeDtypeStruct(blocks, jnp.float32),
            grid_spec=pltpu.PrefetchScalarGridSpec(
                num_scalar_prefetch=1,
                grid=(n_k,),
                in_specs=[
                    pl.BlockSpec((ni, 1, nc, va), lambda k, t: (0, k, 0, 0)),
                    pl.BlockSpec((1, nc, ni, vb), lambda k, t: (k, 0, 0, 0)),
                    pl.BlockSpec((1, nc), lambda k, t: (0, 0)),
                    pl.BlockSpec((nc, 1), lambda k, t: (0, 0)),
                    pl.BlockSpec((1, vb), lambda k, t: (0, 0)),
                ],
                out_specs=pl.BlockSpec(blocks, lambda k, t: (0, 0, 0, 0, 0)),
                scratch_shapes=[
                    pltpu.VMEM((ni, ni * cap, vb), jnp.float32),
                    pltpu.VMEM((ni, va, nc), jnp.float32),
                    pltpu.VMEM((ni * cap, nc), jnp.float32),
                    pltpu.VMEM((ni * cap, 3 * nc), jnp.bfloat16),
                    pltpu.VMEM((ni, 3 * nc, vb), jnp.bfloat16),
                ],
            ),
            compiler_params=pltpu.CompilerParams(vmem_limit_bytes=60 * 2**20),
        )(tab, jnp.swapaxes(amplitudes, 2, 3), cycle_block, c_part[None, :], c_part[:, None], virtual_irreps[None, :])
        _, zs, _, nr, lanes = blocks
        groups = lanes // LANES
        dma = pltpu.SemaphoreType.DMA
        summed = pl.pallas_call(
            exchange,
            out_shape=jax.ShapeDtypeStruct(blocks[2:], jnp.float32),
            in_specs=[pl.BlockSpec(memory_space=pltpu.VMEM)],
            out_specs=pl.BlockSpec(memory_space=pltpu.VMEM),
            scratch_shapes=[
                pltpu.VMEM(blocks[1:], jnp.float32),
                pltpu.VMEM(blocks[1:], jnp.float32),
                pltpu.VMEM((narrow, zs, nr, lanes), jnp.float32),
                pltpu.VMEM((zs, nr, lanes), jnp.float32),
                pltpu.VMEM((zs, nr, lanes), jnp.float32),
                pltpu.VMEM((narrow, nr, lanes), jnp.float32),
                dma((2, groups)),
                dma((narrow, groups)),
                dma((narrow, groups)),
                dma((zs, groups)),
                dma((zs, groups)),
                dma((narrow, groups)),
                dma((narrow, groups)),
            ],
            compiler_params=pltpu.CompilerParams(collective_id=0, has_side_effects=True, vmem_limit_bytes=60 * 2**20),
        )(partial_sums).reshape(ni * bw, lanes)
        low = jnp.maximum(aligned + offset, starts)
        high = jnp.minimum(aligned + offset + cap, ends)
        tab = jnp.concatenate([slab, packed, low, high, b_part[:1], b_part[-1:], (narrow_pos * na)[None]])
        return pl.pallas_call(
            functools.partial(unpack, cap),
            out_shape=jax.ShapeDtypeStruct((ni, ni, na, bw), jnp.float32),
            grid_spec=pltpu.PrefetchScalarGridSpec(
                num_scalar_prefetch=1,
                grid=(1,),
                in_specs=[
                    pl.BlockSpec((ni * bw, ni * cap), lambda k, t: (0, 0)),
                    pl.BlockSpec((1, bw), lambda k, t: (0, 0)),
                ],
                out_specs=pl.BlockSpec((ni, ni, na, bw), lambda k, t: (0, 0, 0, 0)),
                scratch_shapes=[pltpu.VMEM((2 * na + cap, bw), jnp.float32)],
            ),
        )(tab, summed, b_part[None, :])

    first = part(0)
    return lax.cond(jnp.max(ends - aligned) > cap, lambda x: x + part(cap), lambda x: x, first)


def solution(mesh):
    placed = (P(None, "wide", None, "narrow"), P("wide", "narrow", None, None), P(), P(), P())
    return jax.shard_map(
        local,
        mesh=mesh,
        in_specs=placed,
        out_specs=P(None, None, "narrow", "wide"),
        check_vma=False,
    )
```

```python
import functools

import jax
import jax.numpy as jnp
from jax import lax
from jax.experimental import pallas as pl
from jax.experimental.pallas import tpu as pltpu
from jax.sharding import PartitionSpec as P

IRREPS = 8
CORES = 2
LANES = 128
ROWS = 8
FEWEST = 64


def split(x):
    high = x.astype(jnp.bfloat16)
    low = (x - high.astype(jnp.float32)).astype(jnp.bfloat16)
    return high, low


def mm(x, y):
    return jnp.dot(x, y, preferred_element_type=jnp.float32)


def label_of(at, starts):
    return sum((at >= starts[h]).astype(jnp.int32) for h in range(1, IRREPS))


def label_at(at, starts):
    return sum(jnp.where(at >= starts[h], 1, 0) for h in range(1, IRREPS))


def contract(cap, offset, starts, occupied, slab, a_ref, w_ref, out_ref, acc, turn, rows, deep_l, deep_w, labels, c_labels):
    k = pl.program_id(0)
    n_k = pl.num_programs(0)
    ni, nc, va = a_ref.shape[0], a_ref.shape[2], a_ref.shape[3]
    cores, zs, narrow, nr, _ = out_ref.shape
    c0 = lax.axis_index("narrow") * nc
    hk = occupied[lax.axis_index("wide") * n_k + k]
    slab_irreps = [occupied[slab[i]] for i in range(ni)]
    first, last = label_at(c0, starts), label_at(c0 + nc - 1, starts)

    @pl.when(k == 0)
    def _():
        acc[...] = jnp.zeros_like(acc)
        rows[...] = jnp.zeros_like(rows)
        c_labels[...] = label_of(c0 + lax.broadcasted_iota(jnp.int32, c_labels.shape, 1), starts)
        labels[...] = label_of(c0 + lax.broadcasted_iota(jnp.int32, labels.shape, 0), starts) ^ label_of(
            lax.broadcasted_iota(jnp.int32, labels.shape, 1), starts
        )

    for i in range(ni):
        turn[i] = a_ref[i, 0].T

    def pick(h, carry):
        mine = c_labels[...] == h
        for i in range(ni):
            block = h ^ slab_irreps[i] ^ hk
            start = pl.multiple_of(jnp.minimum(starts[block] // ROWS * ROWS + offset, va - cap), ROWS)
            at = slice(i * cap, (i + 1) * cap)
            rows[at, :] = jnp.where(mine, turn[i, pl.ds(start, cap), :], rows[at, :])
        return carry

    lax.fori_loop(first, last + 1, pick, 0)
    l_hi, l_lo = split(rows[...])
    joined = nc % 16 == 0
    if joined:
        deep_l[:, :nc] = l_hi
        deep_l[:, nc : 2 * nc] = l_hi
        deep_l[:, 2 * nc :] = l_lo
    w_all = jnp.swapaxes(w_ref[0], 0, 1)
    for j in range(ni):
        w_hi, w_lo = split(jnp.where(labels[...] == (slab_irreps[j] ^ hk), w_all[j], 0.0))
        if joined:
            deep_w[j, :nc] = w_hi
            deep_w[j, nc : 2 * nc] = w_lo
            deep_w[j, 2 * nc :] = w_hi
            acc[j] += mm(deep_l[...], deep_w[j])
        else:
            acc[j] += mm(l_hi, w_hi) + mm(l_hi, w_lo) + mm(l_lo, w_hi)

    @pl.when(k == n_k - 1)
    def _():
        pieces = narrow // ni
        for j in range(ni):
            turned = acc[j].T
            for n in range(cores * zs * pieces):
                w, piece = divmod(n, pieces)
                out_ref[w % cores, w // cores, j * pieces + piece] = turned[n * nr : (n + 1) * nr]


def exchange(q_ref, out_ref, cbuf, s1, nbuf, s2, zbuf, gbuf, csem, nsend, nrecv, zsend, zrecv, gsend, grecv):
    cores, zs, narrow, _, lanes = q_ref.shape
    wide_pos, n = lax.axis_index("wide"), lax.axis_index("narrow")
    z, core = wide_pos // cores, lax.rem(wide_pos, cores)
    other = 1 - core
    partner = (z * cores + other, n)
    n_peers = [lax.rem(n + d, narrow) for d in range(1, narrow)]
    z_peers = [lax.rem(z + d, zs) for d in range(1, zs)]

    def at_n(p):
        return (wide_pos, p)

    def at_z(p):
        return (p * cores + core, n)

    barrier = pltpu.get_barrier_semaphore()
    peers = [partner] + [at_n(p) for p in n_peers] + [at_z(p) for p in z_peers]
    for peer in peers:
        pl.semaphore_signal(barrier, inc=1, device_id=peer, device_id_type=pl.DeviceIdType.MESH)
    pl.semaphore_wait(barrier, len(peers))

    def copy(src, dst, send, recv, device):
        return pltpu.make_async_remote_copy(
            src_ref=src, dst_ref=dst, send_sem=send, recv_sem=recv, device_id=device, device_id_type=pl.DeviceIdType.MESH
        )

    groups = [(g, pl.ds(g * LANES, LANES)) for g in range(lanes // LANES)]
    sent = []

    def push(c):
        c.start()
        sent.append(c)

    for g, part in groups:
        push(copy(q_ref.at[other, :, :, :, part], cbuf.at[:, :, :, part], csem.at[0, g], csem.at[1, g], partner))
    for g, part in groups:
        sent[g].wait_recv()
        s1[:, :, :, part] = q_ref[core, :, :, :, part] + cbuf[:, :, :, part]
        for p in n_peers:
            push(copy(s1.at[:, p, :, part], nbuf.at[n, :, :, part], nsend.at[p, g], nrecv.at[n, g], at_n(p)))
    for g, part in groups:
        total = s1[:, n, :, part]
        for p in n_peers:
            copy(s1.at[:, p, :, part], nbuf.at[p, :, :, part], nsend.at[p, g], nrecv.at[p, g], at_n(p)).wait_recv()
            total = total + nbuf[p, :, :, part]
        s2[:, :, part] = total
        for p in z_peers:
            push(copy(s2.at[p, :, part], zbuf.at[z, :, part], zsend.at[p, g], zrecv.at[z, g], at_z(p)))
    for g, part in groups:
        total = s2[z, :, part]
        for p in z_peers:
            copy(s2.at[p, :, part], zbuf.at[p, :, part], zsend.at[p, g], zrecv.at[p, g], at_z(p)).wait_recv()
            total = total + zbuf[p, :, part]
        gbuf[n, :, part] = total
        for p in n_peers:
            push(copy(gbuf.at[n, :, part], gbuf.at[n, :, part], gsend.at[p, g], grecv.at[n, g], at_n(p)))
    for g, part in groups:
        for p in n_peers:
            copy(gbuf.at[n, :, part], gbuf.at[p, :, part], gsend.at[p, g], grecv.at[p, g], at_n(p)).wait_recv()
    for c in sent:
        c.wait_send()
    out_ref[...] = gbuf[...]


def unpack(cap, offset, starts, occupied, slab, g_ref, out_ref, buf):
    ni, _, na, bw = out_ref.shape
    va = na * lax.axis_size("narrow")
    buf[...] = jnp.zeros_like(buf)
    slab_irreps = [occupied[slab[i]] for i in range(ni)]
    a0, b0 = lax.axis_index("narrow") * na, lax.axis_index("wide") * bw
    first, last = label_at(b0, starts), label_at(b0 + bw - 1, starts)
    labels = label_of(b0 + lax.broadcasted_iota(jnp.int32, (1, bw), 1), starts)
    at = a0 + lax.broadcasted_iota(jnp.int32, (na, bw), 0)
    for j in range(ni):
        turned = g_ref[j * bw : (j + 1) * bw, :].T
        for i in range(ni):
            buf[na : na + cap, :] = turned[i * cap : (i + 1) * cap]
            g = slab_irreps[i] ^ slab_irreps[j]

            def place(h, kept):
                block = h ^ g
                aligned = starts[block] // ROWS * ROWS + offset
                low = jnp.maximum(aligned, starts[block])
                end = jnp.where(block == IRREPS - 1, va, starts[jnp.minimum(block + 1, IRREPS - 1)])
                high = jnp.minimum(aligned + cap, end)
                start = jnp.clip(na + a0 - jnp.minimum(aligned, va - cap), 0, na + cap)
                use = (labels == h) & (at >= low) & (at < high)
                return jnp.where(use, buf[pl.ds(pl.multiple_of(start, ROWS), na), :], kept)

            out_ref[i, j] = lax.fori_loop(first, last + 1, place, jnp.zeros((na, bw), jnp.float32))


def local(amplitudes, cycle_block, occupied_irreps, virtual_irreps, slab_orbitals):
    ni, n_k, va, nc = amplitudes.shape
    vb = cycle_block.shape[3]
    wide, narrow = lax.axis_size("wide"), lax.axis_size("narrow")
    bw, na = vb // wide, va // narrow
    most = va - (IRREPS - 1) * FEWEST
    cap = most // 2
    blocks = (CORES, wide // CORES, narrow, ni * bw // narrow, ni * cap)

    names = jnp.arange(IRREPS, dtype=jnp.int32)
    starts = jnp.sum((virtual_irreps[None, :] < names[:, None]).astype(jnp.int32), axis=1)
    aligned = starts // ROWS * ROWS
    ends = jnp.concatenate([starts[1:], jnp.full((1,), va, jnp.int32)])

    def part(offset):
        partial_sums = pl.pallas_call(
            functools.partial(contract, cap, offset),
            out_shape=jax.ShapeDtypeStruct(blocks, jnp.float32),
            grid_spec=pltpu.PrefetchScalarGridSpec(
                num_scalar_prefetch=3,
                grid=(n_k,),
                in_specs=[
                    pl.BlockSpec((ni, 1, nc, va), lambda k, *t: (0, k, 0, 0)),
                    pl.BlockSpec((1, nc, ni, vb), lambda k, *t: (k, 0, 0, 0)),
                ],
                out_specs=pl.BlockSpec(blocks, lambda k, *t: (0, 0, 0, 0, 0)),
                scratch_shapes=[
                    pltpu.VMEM((ni, ni * cap, vb), jnp.float32),
                    pltpu.VMEM((ni, va, nc), jnp.float32),
                    pltpu.VMEM((ni * cap, nc), jnp.float32),
                    pltpu.VMEM((ni * cap, 3 * nc), jnp.bfloat16),
                    pltpu.VMEM((ni, 3 * nc, vb), jnp.bfloat16),
                    pltpu.VMEM((nc, vb), jnp.int32),
                    pltpu.VMEM((1, nc), jnp.int32),
                ],
            ),
            compiler_params=pltpu.CompilerParams(vmem_limit_bytes=60 * 2**20),
        )(starts, occupied_irreps, slab_orbitals, jnp.swapaxes(amplitudes, 2, 3), cycle_block)
        _, zs, _, nr, lanes = blocks
        groups = lanes // LANES
        dma = pltpu.SemaphoreType.DMA
        summed = pl.pallas_call(
            exchange,
            out_shape=jax.ShapeDtypeStruct(blocks[2:], jnp.float32),
            in_specs=[pl.BlockSpec(memory_space=pltpu.VMEM)],
            out_specs=pl.BlockSpec(memory_space=pltpu.VMEM),
            scratch_shapes=[
                pltpu.VMEM(blocks[1:], jnp.float32),
                pltpu.VMEM(blocks[1:], jnp.float32),
                pltpu.VMEM((narrow, zs, nr, lanes), jnp.float32),
                pltpu.VMEM((zs, nr, lanes), jnp.float32),
                pltpu.VMEM((zs, nr, lanes), jnp.float32),
                pltpu.VMEM((narrow, nr, lanes), jnp.float32),
                dma((2, groups)),
                dma((narrow, groups)),
                dma((narrow, groups)),
                dma((zs, groups)),
                dma((zs, groups)),
                dma((narrow, groups)),
                dma((narrow, groups)),
            ],
            compiler_params=pltpu.CompilerParams(collective_id=0, has_side_effects=True, vmem_limit_bytes=60 * 2**20),
        )(partial_sums).reshape(ni * bw, lanes)
        return pl.pallas_call(
            functools.partial(unpack, cap, offset),
            out_shape=jax.ShapeDtypeStruct((ni, ni, na, bw), jnp.float32),
            grid_spec=pltpu.PrefetchScalarGridSpec(
                num_scalar_prefetch=3,
                grid=(1,),
                in_specs=[
                    pl.BlockSpec((ni * bw, ni * cap), lambda k, *t: (0, 0)),
                ],
                out_specs=pl.BlockSpec((ni, ni, na, bw), lambda k, *t: (0, 0, 0, 0)),
                scratch_shapes=[pltpu.VMEM((2 * na + cap, bw), jnp.float32)],
            ),
        )(starts, occupied_irreps, slab_orbitals, summed)

    first = part(0)
    return lax.cond(jnp.max(ends - aligned) > cap, lambda x: x + part(cap), lambda x: x, first)


def solution(mesh):
    placed = (P(None, "wide", None, "narrow"), P("wide", "narrow", None, None), P(), P(), P())
    return jax.shard_map(
        local,
        mesh=mesh,
        in_specs=placed,
        out_specs=P(None, None, "narrow", "wide"),
        check_vma=False,
    )
```
